32 devices in a mesh: band: 4 (over x, core), grid: 8 (over z, y).
Axes of the slice: x: 2, y: 2, z: 4, core: 2. Of those that a mesh axis runs over, the one named last changes fastest.
Arguments:
- orbitals: float32 [4, 128, 128, 128], P('band', 'grid'), may hold values from -4 to 10, as said below
- pivots: int32 [4], replicated, may hold values from 0 to 2097151, as said below
- pattern: int32 [4, 4], replicated, may hold values from 0 to 1, as said below
Outputs:
- localized: float32 [4, 128, 128, 128], P('band', 'grid')
- exchange_term: float32 [4, 128, 128, 128], P('band', 'grid')
The draws below stay inside these ranges and needn't reach their ends.
Inputs may be any that keep to these rules, and one draw needn't show every extreme that they name: Values of the orbitals on the grid; the matrix of their values at the pivots has a Cholesky factorization. `pivots`: distinct flat cell indices; the first and the last cell of the grid are always among them. `pattern`: every diagonal entry is 1; each row holds 1 to 4 ones, some row exactly 4; the matrix holds exactly 8 ones.
All inputs are finite; a program needn't handle non-finite values.
Results may differ from the reference program's by a relative error of at most 0.0003.
Values sent between devices are 32-bit elements; how exact they have to be, the bound alone decides.
A program may use at most 64 MiB of HBM per device.

```python
import jax
import jax.numpy as jnp
from jax import lax

BAND_DEV = 1
NG = 128
MOST_PARTNERS = 4
MEAN_PARTNERS = 2
BLOCKS = 4
BANDS = 4


def pivot_cells(key):
    inner_key = jax.random.fold_in(key, 7)
    choose_key, order_key = jax.random.split(inner_key)
    total = NG * NG * NG
    middle = jax.random.choice(choose_key, total - 2, (BANDS - 2,), replace=False).astype(jnp.int32) + 1
    ends = jnp.array([0, total - 1], dtype=jnp.int32)
    joined = jnp.concatenate([ends, middle])
    return jax.random.permutation(order_key, joined).astype(jnp.int32)


def draw_pivots(key, part):
    return pivot_cells(key)


def draw_orbitals(key, part):
    pivot_list = pivot_cells(key)
    key_bulk, key_diag, key_spread = jax.random.split(jax.random.fold_in(key, 11), 3)
    values_bulk = jnp.clip(jax.random.normal(key_bulk, (BANDS, NG * NG * NG), jnp.float32), -4.0, 4.0)
    root_bands = float(BANDS) ** 0.5
    diagonal = jax.random.uniform(key_diag, (BANDS,), jnp.float32, 6.0, 10.0)
    spread = jax.random.uniform(key_spread, (BANDS, BANDS), jnp.float32, -1.0, 1.0) / root_bands
    on_diagonal = jnp.arange(BANDS)[:, None] == jnp.arange(BANDS)[None, :]
    matrix = jnp.where(on_diagonal, diagonal[None, :], spread)
    return values_bulk.at[:, pivot_list].set(matrix).reshape(BANDS, NG, NG, NG)


def draw_pattern(key, part):
    key_heavy, key_order, key_rows = jax.random.split(jax.random.fold_in(key, 23), 3)
    heavy_row = jax.random.randint(key_heavy, (), 0, BLOCKS)
    ordering = jax.random.permutation(key_order, BLOCKS - 1)
    surplus = MEAN_PARTNERS * BLOCKS - BLOCKS - MOST_PARTNERS + 1
    row_ids = jnp.arange(BLOCKS, dtype=jnp.int32)
    position = jnp.clip(jnp.where(row_ids < heavy_row, row_ids, row_ids - 1), 0, BLOCKS - 2)
    counts = jnp.where(row_ids == heavy_row, MOST_PARTNERS, 1 + (ordering[position] < surplus).astype(jnp.int32))

    def one_row(row_id, wanted):
        ranking = jax.random.permutation(jax.random.fold_in(key_rows, row_id), BLOCKS)
        ranking = jnp.where(row_ids == row_id, -1, ranking)
        places = jnp.sum(ranking[None, :] < ranking[:, None], axis=1)
        return (places < wanted).astype(jnp.int32)
    return jax.vmap(one_row)(row_ids, counts)


def setup_inputs(seed: int = 0) -> dict:
    seeds = jax.random.split(jax.random.key(seed), 4)
    orbitals = draw_orbitals(jax.random.fold_in(seeds[3], 71), 0)
    pivots = draw_pivots(jax.random.fold_in(seeds[3], 71), 0)
    pattern = draw_pattern(jax.random.fold_in(seeds[3], 71), 0)
    return dict(orbitals=orbitals, pivots=pivots, pattern=pattern)


precise = lax.Precision.HIGHEST

def wrapped(indices, length):
    return jnp.where(indices < length // 2, indices, indices - length)

def coulomb_kernel(length):
    waves = wrapped(jnp.arange(length, dtype=jnp.int32), length).astype(jnp.float32)
    squared = waves[:, None, None] ** 2 + waves[None, :, None] ** 2 + waves[None, None, :] ** 2
    scaling = float(length) ** 1.5
    return jnp.where(squared > 0, 0.25 / (scaling * jnp.maximum(squared, 1.0)), 0.0)

def reference(orbitals, pivots, pattern):
    flat_orbitals = orbitals.reshape(BANDS, NG * NG * NG)
    picked = jnp.take(flat_orbitals, pivots, axis=1)
    gram_matrix = jnp.dot(picked.T, picked, precision=precise)
    factor = jnp.linalg.cholesky(gram_matrix)
    rotation = lax.linalg.triangular_solve(factor, picked.T, left_side=True, lower=True).T
    localized = jnp.dot(rotation.T, flat_orbitals, precision=precise).reshape(BANDS, NG, NG, NG)
    kernel = coulomb_kernel(NG)
    volume = float(NG) ** 3
    band_block = jnp.arange(BANDS, dtype=jnp.int32) // BAND_DEV
    weights = pattern[band_block[:, None], band_block[None, :]].astype(localized.dtype)

    def one_band(inputs):
        single, weight_row = inputs
        density = single[None] * localized
        spectra = jnp.fft.fftn(density, axes=(1, 2, 3)) * kernel
        potential = jnp.real(jnp.fft.ifftn(spectra, axes=(1, 2, 3))) * volume
        return jnp.sum(weight_row[:, None, None, None] * potential * localized, axis=0)
    exchange_term = lax.map(one_band, (localized, weights))
    return (localized, exchange_term)
```

```python
import jax
import jax.numpy as jnp
from jax import lax
from jax.sharding import PartitionSpec as P

precise = lax.Precision.HIGHEST
swift = lax.Precision.HIGHEST


def tables(length):
    across = jnp.arange(length, dtype=jnp.int32)
    phases = across[:, None] * across[None, :] % length
    angles = phases.astype(jnp.float32) * (2.0 * jnp.pi / length)
    return (jnp.cos(angles), jnp.sin(angles))


def wrapped(indices, length):
    return jnp.where(indices < length // 2, indices, indices - length)


def coulomb(length, plane_start, plane_count):
    wave_first = wrapped(jnp.arange(length, dtype=jnp.int32), length).astype(jnp.float32)
    wave_second = wrapped(plane_start + jnp.arange(plane_count, dtype=jnp.int32), length).astype(
        jnp.float32
    )
    squared = (
        wave_first[:, None, None] ** 2
        + wave_second[None, :, None] ** 2
        + wave_first[None, None, :] ** 2
    )
    scaling = float(length) ** 1.5
    return jnp.where(squared > 0, 0.25 / (scaling * jnp.maximum(squared, 1.0)), 0.0)


def filtered(real_in, imag_in, kernel, cos_table, sin_table):
    real_part = jnp.dot(real_in, cos_table, precision=swift) + jnp.dot(
        imag_in, sin_table, precision=swift
    )
    imag_part = jnp.dot(imag_in, cos_table, precision=swift) - jnp.dot(
        real_in, sin_table, precision=swift
    )
    real_part, imag_part = (
        jnp.einsum("pxyz,yk->pxkz", real_part, cos_table, precision=swift)
        + jnp.einsum("pxyz,yk->pxkz", imag_part, sin_table, precision=swift),
        jnp.einsum("pxyz,yk->pxkz", imag_part, cos_table, precision=swift)
        - jnp.einsum("pxyz,yk->pxkz", real_part, sin_table, precision=swift),
    )
    real_wide = lax.all_to_all(real_part, "grid", split_axis=2, concat_axis=1, tiled=True)
    imag_wide = lax.all_to_all(imag_part, "grid", split_axis=2, concat_axis=1, tiled=True)
    ahead_real = (
        jnp.einsum("pxyz,xk->pkyz", real_wide, cos_table, precision=swift)
        + jnp.einsum("pxyz,xk->pkyz", imag_wide, sin_table, precision=swift)
    ) * kernel
    ahead_imag = (
        jnp.einsum("pxyz,xk->pkyz", imag_wide, cos_table, precision=swift)
        - jnp.einsum("pxyz,xk->pkyz", real_wide, sin_table, precision=swift)
    ) * kernel
    back_real = jnp.einsum("pxyz,xk->pkyz", ahead_real, cos_table, precision=swift) - jnp.einsum(
        "pxyz,xk->pkyz", ahead_imag, sin_table, precision=swift
    )
    back_imag = jnp.einsum("pxyz,xk->pkyz", ahead_imag, cos_table, precision=swift) + jnp.einsum(
        "pxyz,xk->pkyz", ahead_real, sin_table, precision=swift
    )
    real_part = lax.all_to_all(back_real, "grid", split_axis=1, concat_axis=2, tiled=True)
    imag_part = lax.all_to_all(back_imag, "grid", split_axis=1, concat_axis=2, tiled=True)
    real_part, imag_part = (
        jnp.einsum("pxyz,yk->pxkz", real_part, cos_table, precision=swift)
        - jnp.einsum("pxyz,yk->pxkz", imag_part, sin_table, precision=swift),
        jnp.einsum("pxyz,yk->pxkz", imag_part, cos_table, precision=swift)
        + jnp.einsum("pxyz,yk->pxkz", real_part, sin_table, precision=swift),
    )
    out_real = jnp.dot(real_part, cos_table, precision=swift) - jnp.dot(
        imag_part, sin_table, precision=swift
    )
    out_imag = jnp.dot(imag_part, cos_table, precision=swift) + jnp.dot(
        real_part, sin_table, precision=swift
    )
    return (out_real, out_imag)


def assignment(pattern):
    blocks = pattern.shape[0]
    ids = jnp.arange(blocks, dtype=jnp.int32)
    off = ((pattern == 1) & (ids[:, None] != ids[None, :])).astype(jnp.int32).reshape(-1)
    before = jnp.cumsum(off) - off
    chosen = (off[None, :] == 1) & (before[None, :] == ids[:, None])
    chosen = chosen.reshape(blocks, blocks, blocks)
    firsts = jnp.any(chosen, axis=2).astype(jnp.float32)
    seconds = jnp.any(chosen, axis=1).astype(jnp.float32)
    return firsts, seconds


def mixed(coefficients, bands):
    total = coefficients[0] * bands[0]
    for band in range(1, bands.shape[0]):
        total = total + coefficients[band] * bands[band]
    return total


def local(orbitals, pivots, pattern):
    slab_planes = orbitals.shape[1]
    length = orbitals.shape[3]
    block_total = pattern.shape[0]
    grid_index = lax.axis_index("grid")
    band_index = lax.axis_index("band")
    every = lax.all_gather(orbitals, "band", axis=0, tiled=True)
    local_cell = pivots - grid_index * (slab_planes * length * length)
    inside = (local_cell >= 0) & (local_cell < slab_planes * length * length)
    cell = jnp.clip(local_cell, 0, slab_planes * length * length - 1)
    rows = jnp.take(orbitals.reshape(slab_planes * length, length), cell // length, axis=0)
    lanes = jnp.arange(length, dtype=jnp.int32)
    sampled = jnp.sum(jnp.where(lanes[None, :] == (cell % length)[:, None], rows, 0.0), axis=1)
    own = jnp.where(inside, sampled, 0.0)
    ids = jnp.arange(block_total, dtype=jnp.int32)
    picked = lax.psum(
        jnp.where(ids[:, None] == band_index, own[None, :], 0.0), ("band", "grid")
    )
    gram_matrix = jnp.dot(picked.T, picked, precision=precise)
    factor = jnp.linalg.cholesky(gram_matrix)
    rotation = lax.linalg.triangular_solve(factor, picked.T, left_side=True, lower=True).T
    firsts, seconds = assignment(pattern)
    selectors = jnp.stack(
        [
            (ids == band_index).astype(jnp.float32),
            lax.dynamic_index_in_dim(firsts, band_index, 0, keepdims=False),
            lax.dynamic_index_in_dim(seconds, band_index, 0, keepdims=False),
        ]
    )
    coefficients = jnp.dot(selectors, rotation.T, precision=precise)
    localized = mixed(coefficients[0], every)
    first = mixed(coefficients[1], every)
    second = mixed(coefficients[2], every)
    cos_table, sin_table = tables(length)
    plane_count = length // lax.axis_size("grid")
    kernel = coulomb(length, grid_index * plane_count, plane_count)
    potential_own, potential_off = filtered(
        (localized * localized)[None], (first * second)[None], kernel, cos_table, sin_table
    )
    terms = lax.all_gather(potential_off[0] * second, "band", axis=0, tiled=False)
    weights = lax.dynamic_index_in_dim(firsts, band_index, 1, keepdims=False)
    exchange_term = potential_own[0] * localized + mixed(weights, terms)
    return (localized[None], exchange_term[None])


def solution(mesh):
    return jax.shard_map(
        local,
        mesh=mesh,
        in_specs=(P("band", "grid", None, None), P(), P()),
        out_specs=(P("band", "grid", None, None), P("band", "grid", None, None)),
        check_vma=False,
    )
```

```python
import functools

import jax
import jax.numpy as jnp
import numpy as np
from jax import lax
from jax.experimental import pallas as pl
from jax.experimental.pallas import tpu as pltpu
from jax.sharding import PartitionSpec as P

precise = lax.Precision.HIGHEST
MESH = pl.DeviceIdType.MESH


def complex_table(length):
    across = np.arange(length)
    angles = (across[:, None] * across[None, :] % length) * (2.0 * np.pi / length)
    cosine, sine = np.cos(angles), np.sin(angles)
    return np.block([[cosine, -sine], [sine, cosine]]).astype(np.float32)


def wrapped(indices, length):
    return jnp.where(indices < length // 2, indices, indices - length)


def coulomb(length, row_start, row_count):
    wave = wrapped(jnp.arange(length, dtype=jnp.int32), length).astype(jnp.float32)
    rows = wrapped(row_start + jnp.arange(row_count, dtype=jnp.int32), length).astype(jnp.float32)
    squared = rows[:, None, None] ** 2 + wave[None, :, None] ** 2 + wave[None, None, :] ** 2
    scaling = float(length) ** 1.5
    return jnp.where(squared > 0, 0.25 / (scaling * jnp.maximum(squared, 1.0)), 0.0)


def times(left, right):
    return jnp.dot(left, right, precision=precise, preferred_element_type=jnp.float32)


def transform_kernel(
    n, halves, chunks,
    own_ref, first_ref, second_ref, kern_ref, fwd_ref, bwd_ref,
    term_ref, off_ref,
    send_one, recv_one, send_two, recv_two,
    sems_one_send, sems_one_recv, sems_two_send, sems_two_recv, sems_own,
):
    planes, length = own_ref.shape[0], own_ref.shape[2]
    depth = length // n
    rows = depth // halves
    chunk = planes // chunks
    me = lax.axis_index("grid")
    barrier = pltpu.get_barrier_semaphore()
    for step in range(1, n):
        pl.semaphore_signal(
            barrier, inc=1, device_id={"grid": lax.rem(me + step, n)}, device_id_type=MESH
        )
    pl.semaphore_wait(barrier, n - 1)

    def out_copies(part, half):
        size = chunk * rows
        mine = pl.ds(pl.multiple_of(me * (planes * rows) + part * size, size), size)
        copies = []
        for step in range(1, n):
            target = lax.rem(me + step, n)
            copies.append(
                pltpu.make_async_remote_copy(
                    src_ref=send_one.at[target, half, :, pl.ds(part * size, size), :],
                    dst_ref=recv_one.at[half, :, mine, :],
                    send_sem=sems_one_send.at[part, half, step],
                    recv_sem=sems_one_recv.at[part, half, step],
                    device_id={"grid": target},
                    device_id_type=MESH,
                )
            )
        return copies

    def own_copy(half):
        size = planes * rows
        return pltpu.make_async_copy(
            send_one.at[me, half],
            recv_one.at[half, :, pl.ds(pl.multiple_of(me * size, size), size), :],
            sems_own.at[half],
        )

    def back_copies(half):
        size = planes * rows
        copies = []
        for step in range(1, n):
            target = lax.rem(me + step, n)
            copies.append(
                pltpu.make_async_remote_copy(
                    src_ref=send_two.at[half, :, pl.ds(pl.multiple_of(target * size, size), size), :],
                    dst_ref=recv_two.at[half, me],
                    send_sem=sems_two_send.at[half, step],
                    recv_sem=sems_two_recv.at[half, step],
                    device_id={"grid": target},
                    device_id_type=MESH,
                )
            )
        return copies

    def own_back(half):
        size = planes * rows
        return pltpu.make_async_copy(
            send_two.at[half, :, pl.ds(pl.multiple_of(me * size, size), size), :],
            recv_two.at[half, me],
            sems_own.at[halves + half],
        )

    def ahead(pair, carry):
        pieces = []
        for which in range(2):
            plane = pair * 2 + which
            own = own_ref[plane]
            both = jnp.concatenate([own * own, first_ref[plane] * second_ref[plane]], axis=1)
            spectrum = times(both, fwd_ref[...])
            pieces.append(
                jnp.concatenate([spectrum[:, :length], spectrum[:, length:]], axis=0)
            )
        result = times(bwd_ref[...], jnp.concatenate(pieces, axis=1))
        for which in range(2):
            for target in range(n):
                for half in range(halves):
                    for part in range(2):
                        low = part * length + target * depth + half * rows
                        send_one[target, half, part, pl.ds((pair * 2 + which) * rows, rows), :] = (
                            result[low : low + rows, which * length : (which + 1) * length]
                        )
        return carry

    for part in range(chunks):
        lax.fori_loop(part * chunk // 2, (part + 1) * chunk // 2, ahead, 0)
        for copy in out_copies(part, 0):
            copy.start()
    for half in range(1, halves):
        for part in range(chunks):
            for copy in out_copies(part, half):
                copy.start()
    for half in range(halves):
        own_copy(half).start()

    for half in range(halves):
        own_copy(half).wait()
        for part in range(chunks):
            for copy in out_copies(part, half):
                copy.wait_recv()

        def columns(pair, carry):
            pieces = []
            for which in range(2):
                place = pl.ds(pair * 2 + which, length, stride=rows)
                pieces.append(
                    jnp.concatenate(
                        [recv_one[half, 0, place, :], recv_one[half, 1, place, :]], axis=0
                    )
                )
            spectrum = times(bwd_ref[...], jnp.concatenate(pieces, axis=1))
            weights = jnp.concatenate(
                [kern_ref[half * rows + pair * 2], kern_ref[half * rows + pair * 2 + 1]], axis=1
            )
            spectrum = spectrum * jnp.concatenate([weights, weights], axis=0)
            result = times(fwd_ref[...], spectrum)
            for which in range(2):
                place = pl.ds(pair * 2 + which, length, stride=rows)
                lanes = slice(which * length, (which + 1) * length)
                send_two[half, 0, place, :] = result[:length, lanes]
                send_two[half, 1, place, :] = result[length:, lanes]
            return carry

        lax.fori_loop(0, rows // 2, columns, 0)
        for copy in back_copies(half):
            copy.start()
        own_back(half).start()

    for half in range(halves):
        own_back(half).wait()
        for copy in back_copies(half):
            copy.wait_recv()

    def home(pair, carry):
        pieces = []
        for which in range(2):
            place = pl.ds((pair * 2 + which) * rows, rows)
            pieces.append(
                jnp.concatenate(
                    [
                        recv_two[half, source, part, place, :]
                        for part in range(2)
                        for source in range(n)
                        for half in range(halves)
                    ],
                    axis=0,
                )
            )
        result = times(fwd_ref[...], jnp.concatenate(pieces, axis=1))
        for which in range(2):
            plane = pair * 2 + which
            lanes = slice(which * length, (which + 1) * length)
            both = jnp.concatenate([result[:length, lanes], result[length:, lanes]], axis=1)
            potential = times(both, bwd_ref[...])
            term_ref[plane] = potential[:, :length] * own_ref[plane]
            off_ref[plane] = potential[:, length:] * second_ref[plane]
        return carry

    lax.fori_loop(0, planes // 2, home, 0)
    for half in range(halves):
        for part in range(chunks):
            for copy in out_copies(part, half):
                copy.wait_send()
        for copy in back_copies(half):
            copy.wait_send()


def terms_of(own, first, second, kernel):
    n = lax.axis_size("grid")
    planes, length = own.shape[0], own.shape[2]
    depth = length // n
    halves = 2 if depth % 16 == 0 else 1
    rows = depth // halves
    chunk = max(planes // 4, 2)
    chunks = planes // chunk
    forward = complex_table(length)
    vmem = pl.BlockSpec(memory_space=pltpu.VMEM)
    slab = jax.ShapeDtypeStruct(own.shape, jnp.float32)
    block = planes * rows
    return pl.pallas_call(
        functools.partial(transform_kernel, n, halves, chunks),
        out_shape=(slab, slab),
        in_specs=[vmem] * 6,
        out_specs=(vmem, vmem),
        scratch_shapes=[
            pltpu.VMEM((n, halves, 2, block, length), jnp.float32),
            pltpu.VMEM((halves, 2, n * block, length), jnp.float32),
            pltpu.VMEM((halves, 2, n * block, length), jnp.float32),
            pltpu.VMEM((halves, n, 2, block, length), jnp.float32),
            pltpu.SemaphoreType.DMA((chunks, halves, n)),
            pltpu.SemaphoreType.DMA((chunks, halves, n)),
            pltpu.SemaphoreType.DMA((halves, n)),
            pltpu.SemaphoreType.DMA((halves, n)),
            pltpu.SemaphoreType.DMA((2 * halves,)),
        ],
        compiler_params=pltpu.CompilerParams(
            collective_id=0, has_side_effects=True, vmem_limit_bytes=40 * 1024 * 1024
        ),
    )(own, first, second, kernel, jnp.asarray(forward), jnp.asarray(forward.T.copy()))


def assignment(pattern):
    blocks = pattern.shape[0]
    ids = jnp.arange(blocks, dtype=jnp.int32)
    off = ((pattern == 1) & (ids[:, None] != ids[None, :])).astype(jnp.int32).reshape(-1)
    before = jnp.cumsum(off) - off
    chosen = (off[None, :] == 1) & (before[None, :] == ids[:, None])
    chosen = chosen.reshape(blocks, blocks, blocks)
    firsts = jnp.any(chosen, axis=2).astype(jnp.float32)
    seconds = jnp.any(chosen, axis=1).astype(jnp.float32)
    return firsts, seconds


def mixed(coefficients, bands):
    total = coefficients[0] * bands[0]
    for band in range(1, bands.shape[0]):
        total = total + coefficients[band] * bands[band]
    return total


def local(orbitals, pivots, pattern):
    slab_planes = orbitals.shape[1]
    length = orbitals.shape[3]
    block_total = pattern.shape[0]
    grid_index = lax.axis_index("grid")
    band_index = lax.axis_index("band")
    every = lax.all_gather(orbitals, "band", axis=0, tiled=True)
    local_cell = pivots - grid_index * (slab_planes * length * length)
    inside = (local_cell >= 0) & (local_cell < slab_planes * length * length)
    cell = jnp.clip(local_cell, 0, slab_planes * length * length - 1)
    rows = jnp.take(orbitals.reshape(slab_planes * length, length), cell // length, axis=0)
    lanes = jnp.arange(length, dtype=jnp.int32)
    sampled = jnp.sum(jnp.where(lanes[None, :] == (cell % length)[:, None], rows, 0.0), axis=1)
    own = jnp.where(inside, sampled, 0.0)
    ids = jnp.arange(block_total, dtype=jnp.int32)
    picked = lax.psum(
        jnp.where(ids[:, None] == band_index, own[None, :], 0.0), ("band", "grid")
    )
    gram_matrix = jnp.dot(picked.T, picked, precision=precise)
    factor = jnp.linalg.cholesky(gram_matrix)
    rotation = lax.linalg.triangular_solve(factor, picked.T, left_side=True, lower=True).T
    firsts, seconds = assignment(pattern)
    selectors = jnp.stack(
        [
            (ids == band_index).astype(jnp.float32),
            lax.dynamic_index_in_dim(firsts, band_index, 0, keepdims=False),
            lax.dynamic_index_in_dim(seconds, band_index, 0, keepdims=False),
        ]
    )
    coefficients = jnp.dot(selectors, rotation.T, precision=precise)
    localized = mixed(coefficients[0], every)
    first = mixed(coefficients[1], every)
    second = mixed(coefficients[2], every)
    depth = length // lax.axis_size("grid")
    kernel = coulomb(length, grid_index * depth, depth)
    own_term, off_term = terms_of(localized, first, second, kernel)
    terms = lax.all_gather(off_term, "band", axis=0, tiled=False)
    weights = lax.dynamic_index_in_dim(firsts, band_index, 1, keepdims=False)
    exchange_term = own_term + mixed(weights, terms)
    return (localized[None], exchange_term[None])


def solution(mesh):
    return jax.shard_map(
        local,
        mesh=mesh,
        in_specs=(P("band", "grid", None, None), P(), P()),
        out_specs=(P("band", "grid", None, None), P("band", "grid", None, None)),
        check_vma=False,
    )
```

```python
import functools

import jax
import jax.numpy as jnp
import numpy as np
from jax import lax
from jax.experimental import pallas as pl
from jax.experimental.pallas import tpu as pltpu
from jax.sharding import PartitionSpec as P

precise = lax.Precision.HIGHEST
MESH = pl.DeviceIdType.MESH


def complex_table(length):
    across = np.arange(length)
    angles = (across[:, None] * across[None, :] % length) * (2.0 * np.pi / length)
    cosine, sine = np.cos(angles), np.sin(angles)
    return np.block([[cosine, -sine], [sine, cosine]]).astype(np.float32)


def wrapped(indices, length):
    return jnp.where(indices < length // 2, indices, indices - length)


def coulomb(length, row_start, row_count):
    wave = wrapped(jnp.arange(length, dtype=jnp.int32), length).astype(jnp.float32)
    rows = wrapped(row_start + jnp.arange(row_count, dtype=jnp.int32), length).astype(jnp.float32)
    squared = rows[:, None, None] ** 2 + wave[None, :, None] ** 2 + wave[None, None, :] ** 2
    scaling = float(length) ** 1.5
    return jnp.where(squared > 0, 0.25 / (scaling * jnp.maximum(squared, 1.0)), 0.0)


def times(left, right):
    return jnp.dot(left, right, precision=precise, preferred_element_type=jnp.float32)


def sum_kernel(n, bands, own_ref, out_ref, wide, from_grid, from_band, sems):
    grid_me, band_me = lax.axis_index("grid"), lax.axis_index("band")
    barrier = pltpu.get_barrier_semaphore()
    axes = (("grid", n, grid_me), ("band", bands, band_me))
    for axis, count, me in axes:
        for step in range(1, count):
            pl.semaphore_signal(
                barrier, inc=1, device_id={axis: lax.rem(me + step, count)}, device_id_type=MESH
            )
    pl.semaphore_wait(barrier, n + bands - 2)
    total = own_ref[...]
    for place, (axis, count, me) in enumerate(axes):
        wide[place] = total
        landing = (from_grid, from_band)[place]
        copies = []
        for step in range(1, count):
            copy = pltpu.make_async_remote_copy(
                src_ref=wide.at[place],
                dst_ref=landing.at[step],
                send_sem=sems.at[place, 0, step],
                recv_sem=sems.at[place, 1, step],
                device_id={axis: lax.rem(me + step, count)},
                device_id_type=MESH,
            )
            copy.start()
            copies.append(copy)
        for step, copy in enumerate(copies):
            copy.wait()
            total = total + landing[step + 1]
    out_ref[...] = total


def summed(table):
    n, bands = lax.axis_size("grid"), lax.axis_size("band")
    tile = (-(-table.shape[0] // 8) * 8, 128)
    vmem = pl.BlockSpec(memory_space=pltpu.VMEM)
    padded = jnp.pad(
        table, ((0, tile[0] - table.shape[0]), (0, tile[1] - table.shape[1]))
    )
    result = pl.pallas_call(
        functools.partial(sum_kernel, n, bands),
        out_shape=jax.ShapeDtypeStruct(tile, jnp.float32),
        in_specs=[vmem],
        out_specs=vmem,
        scratch_shapes=[
            pltpu.VMEM((2,) + tile, jnp.float32),
            pltpu.VMEM((n,) + tile, jnp.float32),
            pltpu.VMEM((bands,) + tile, jnp.float32),
            pltpu.SemaphoreType.DMA((2, 2, max(n, bands))),
        ],
        compiler_params=pltpu.CompilerParams(collective_id=1, has_side_effects=True),
    )(padded)
    return result[: table.shape[0], : table.shape[1]]


def transform_kernel(
    n, halves, chunks, chips,
    mix_ref, share_ref, every_ref, kern_ref, fwd_ref, bwd_ref,
    own_ref, term_ref,
    send_one, recv_one, send_two, recv_two, second_ref, off_ref, twin_ref, going, coming,
    sems_one_send, sems_one_recv, sems_two_send, sems_two_recv, sems_own, sems_twin, sems_chip,
):
    bands = every_ref.shape[0]
    planes, length = own_ref.shape[0], own_ref.shape[2]
    band_me = lax.axis_index("band")
    chip, core = band_me // 2, lax.rem(band_me, 2)
    partner = chip * 2 + 1 - core
    peers = [lax.rem(chip + step, chips) * 2 + core for step in range(1, chips)]
    depth = length // n
    rows = depth // halves
    chunk = planes // chunks
    me = lax.axis_index("grid")
    barrier = pltpu.get_barrier_semaphore()
    for step in range(1, n):
        pl.semaphore_signal(
            barrier, inc=1, device_id={"grid": lax.rem(me + step, n)}, device_id_type=MESH
        )
    for peer in [partner] + peers:
        pl.semaphore_signal(barrier, inc=1, device_id={"band": peer}, device_id_type=MESH)
    pl.semaphore_wait(barrier, n - 1 + chips)

    def out_copies(part, half):
        size = chunk * rows
        mine = pl.ds(pl.multiple_of(me * (planes * rows) + part * size, size), size)
        copies = []
        for step in range(1, n):
            target = lax.rem(me + step, n)
            copies.append(
                pltpu.make_async_remote_copy(
                    src_ref=send_one.at[target, half, :, pl.ds(part * size, size), :],
                    dst_ref=recv_one.at[half, :, mine, :],
                    send_sem=sems_one_send.at[part, half, step],
                    recv_sem=sems_one_recv.at[part, half, step],
                    device_id={"grid": target},
                    device_id_type=MESH,
                )
            )
        return copies

    def own_copy(half):
        size = planes * rows
        return pltpu.make_async_copy(
            send_one.at[me, half],
            recv_one.at[half, :, pl.ds(pl.multiple_of(me * size, size), size), :],
            sems_own.at[half],
        )

    def back_copies(half, part):
        size = planes * rows
        step_size = chunk * rows
        copies = []
        for step in range(1, n):
            target = lax.rem(me + step, n)
            start = pl.multiple_of(target * size + part * step_size, step_size)
            copies.append(
                pltpu.make_async_remote_copy(
                    src_ref=send_two.at[half, :, pl.ds(start, step_size), :],
                    dst_ref=recv_two.at[half, me, :, pl.ds(part * step_size, step_size), :],
                    send_sem=sems_two_send.at[part, half, step],
                    recv_sem=sems_two_recv.at[part, half, step],
                    device_id={"grid": target},
                    device_id_type=MESH,
                )
            )
        return copies

    def own_back(half):
        size = planes * rows
        return pltpu.make_async_copy(
            send_two.at[half, :, pl.ds(pl.multiple_of(me * size, size), size), :],
            recv_two.at[half, me],
            sems_own.at[halves + half],
        )

    def ahead(pair, carry):
        pieces = []
        for which in range(2):
            plane = pair * 2 + which
            values = [every_ref[band, plane] for band in range(bands)]
            own, first, second = [
                sum(mix_ref[kind, band] * values[band] for band in range(1, bands))
                + mix_ref[kind, 0] * values[0]
                for kind in range(3)
            ]
            own_ref[plane] = own
            second_ref[plane] = second
            both = jnp.concatenate([own * own, first * second], axis=1)
            spectrum = times(both, fwd_ref[...])
            pieces.append(
                jnp.concatenate([spectrum[:, :length], spectrum[:, length:]], axis=0)
            )
        result = times(bwd_ref[...], jnp.concatenate(pieces, axis=1))
        for which in range(2):
            for target in range(n):
                for half in range(halves):
                    for part in range(2):
                        low = part * length + target * depth + half * rows
                        send_one[target, half, part, pl.ds((pair * 2 + which) * rows, rows), :] = (
                            result[low : low + rows, which * length : (which + 1) * length]
                        )
        return carry

    for part in range(chunks):
        lax.fori_loop(part * chunk // 2, (part + 1) * chunk // 2, ahead, 0)
        for copy in out_copies(part, 0):
            copy.start()
    for half in range(1, halves):
        for part in range(chunks):
            for copy in out_copies(part, half):
                copy.start()
    for half in range(halves):
        own_copy(half).start()

    for half in range(halves):
        own_copy(half).wait()
        for part in range(chunks):
            for copy in out_copies(part, half):
                copy.wait_recv()

        def columns(pair, carry):
            pieces = []
            for which in range(2):
                place = pl.ds(pair * 2 + which, length, stride=rows)
                pieces.append(
                    jnp.concatenate(
                        [recv_one[half, 0, place, :], recv_one[half, 1, place, :]], axis=0
                    )
                )
            spectrum = times(bwd_ref[...], jnp.concatenate(pieces, axis=1))
            weights = jnp.concatenate(
                [kern_ref[half * rows + pair * 2], kern_ref[half * rows + pair * 2 + 1]], axis=1
            )
            spectrum = spectrum * jnp.concatenate([weights, weights], axis=0)
            result = times(fwd_ref[...], spectrum)
            for which in range(2):
                place = pl.ds(pair * 2 + which, length, stride=rows)
                lanes = slice(which * length, (which + 1) * length)
                send_two[half, 0, place, :] = result[:length, lanes]
                send_two[half, 1, place, :] = result[length:, lanes]
            return carry

        lax.fori_loop(0, rows // 2, columns, 0)
        for part in range(chunks):
            for copy in back_copies(half, part):
                copy.start()
        own_back(half).start()

    for half in range(halves):
        own_back(half).wait()

    def twin_copy(part):
        place = pl.ds(part * chunk, chunk)
        return pltpu.make_async_remote_copy(
            src_ref=off_ref.at[place],
            dst_ref=twin_ref.at[place],
            send_sem=sems_twin.at[0, part],
            recv_sem=sems_twin.at[1, part],
            device_id={"band": partner},
            device_id_type=MESH,
        )

    def chip_copies(part):
        place = pl.ds(part * chunk, chunk)
        return [
            pltpu.make_async_remote_copy(
                src_ref=going.at[step, place],
                dst_ref=coming.at[step, place],
                send_sem=sems_chip.at[0, part, step],
                recv_sem=sems_chip.at[1, part, step],
                device_id={"band": peer},
                device_id_type=MESH,
            )
            for step, peer in enumerate(peers)
        ]

    def shared(part):
        twin_copy(part).wait_recv()

        def one(plane, carry):
            mine, other = off_ref[plane], twin_ref[plane]
            for step, peer in enumerate(peers):
                going[step, plane] = (
                    share_ref[band_me, peer] * mine + share_ref[partner, peer] * other
                )
            term_ref[plane] = (
                term_ref[plane]
                + share_ref[band_me, band_me] * mine
                + share_ref[partner, band_me] * other
            )
            return carry

        lax.fori_loop(part * chunk, (part + 1) * chunk, one, 0)
        for copy in chip_copies(part):
            copy.start()

    def home(pair, carry):
        pieces = []
        for which in range(2):
            place = pl.ds((pair * 2 + which) * rows, rows)
            pieces.append(
                jnp.concatenate(
                    [
                        recv_two[half, source, part, place, :]
                        for part in range(2)
                        for source in range(n)
                        for half in range(halves)
                    ],
                    axis=0,
                )
            )
        result = times(fwd_ref[...], jnp.concatenate(pieces, axis=1))
        for which in range(2):
            plane = pair * 2 + which
            lanes = slice(which * length, (which + 1) * length)
            both = jnp.concatenate([result[:length, lanes], result[length:, lanes]], axis=1)
            potential = times(both, bwd_ref[...])
            term_ref[plane] = potential[:, :length] * own_ref[plane]
            off_ref[plane] = potential[:, length:] * second_ref[plane]
        return carry

    for part in range(chunks):
        for half in range(halves):
            for copy in back_copies(half, part):
                copy.wait_recv()
        lax.fori_loop(part * chunk // 2, (part + 1) * chunk // 2, home, 0)
        twin_copy(part).start()
        if part > 0:
            shared(part - 1)
    shared(chunks - 1)

    def last(plane, carry):
        total = term_ref[plane]
        for step in range(chips - 1):
            total = total + coming[step, plane]
        term_ref[plane] = total
        return carry

    for part in range(chunks):
        for copy in chip_copies(part):
            copy.wait()
        lax.fori_loop(part * chunk, (part + 1) * chunk, last, 0)
        twin_copy(part).wait_send()
    for half in range(halves):
        for part in range(chunks):
            for copy in out_copies(part, half):
                copy.wait_send()
            for copy in back_copies(half, part):
                copy.wait_send()


def exchanged(mix, share, every, kernel):
    n = lax.axis_size("grid")
    planes, length = every.shape[1], every.shape[3]
    chips = lax.axis_size("band") // 2
    depth = length // n
    halves = 2 if depth % 16 == 0 else 1
    rows = depth // halves
    chunk = max(planes // 4, 2)
    chunks = planes // chunk
    forward = complex_table(length)
    vmem = pl.BlockSpec(memory_space=pltpu.VMEM)
    smem = pl.BlockSpec(memory_space=pltpu.SMEM)
    slab = jax.ShapeDtypeStruct(every.shape[1:], jnp.float32)
    block = planes * rows
    return pl.pallas_call(
        functools.partial(transform_kernel, n, halves, chunks, chips),
        out_shape=(slab, slab),
        in_specs=[smem] * 2 + [vmem] * 4,
        out_specs=(vmem, vmem),
        scratch_shapes=[
            pltpu.VMEM((n, halves, 2, block, length), jnp.float32),
            pltpu.VMEM((halves, 2, n * block, length), jnp.float32),
            pltpu.VMEM((halves, 2, n * block, length), jnp.float32),
            pltpu.VMEM((halves, n, 2, block, length), jnp.float32),
            pltpu.VMEM(slab.shape, jnp.float32),
            pltpu.VMEM(slab.shape, jnp.float32),
            pltpu.VMEM(slab.shape, jnp.float32),
            pltpu.VMEM((chips - 1,) + slab.shape, jnp.float32),
            pltpu.VMEM((chips - 1,) + slab.shape, jnp.float32),
            pltpu.SemaphoreType.DMA((chunks, halves, n)),
            pltpu.SemaphoreType.DMA((chunks, halves, n)),
            pltpu.SemaphoreType.DMA((chunks, halves, n)),
            pltpu.SemaphoreType.DMA((chunks, halves, n)),
            pltpu.SemaphoreType.DMA((2 * halves,)),
            pltpu.SemaphoreType.DMA((2, chunks)),
            pltpu.SemaphoreType.DMA((2, chunks, max(chips - 1, 1))),
        ],
        compiler_params=pltpu.CompilerParams(
            collective_id=0, has_side_effects=True, vmem_limit_bytes=40 * 1024 * 1024
        ),
    )(mix, share, every, kernel, jnp.asarray(forward), jnp.asarray(forward.T.copy()))


def assignment(pattern):
    blocks = pattern.shape[0]
    ids = jnp.arange(blocks, dtype=jnp.int32)
    off = ((pattern == 1) & (ids[:, None] != ids[None, :])).astype(jnp.int32).reshape(-1)
    before = jnp.cumsum(off) - off
    chosen = (off[None, :] == 1) & (before[None, :] == ids[:, None])
    chosen = chosen.reshape(blocks, blocks, blocks)
    firsts = jnp.any(chosen, axis=2).astype(jnp.float32)
    seconds = jnp.any(chosen, axis=1).astype(jnp.float32)
    return firsts, seconds


def local(orbitals, pivots, pattern):
    slab_planes = orbitals.shape[1]
    length = orbitals.shape[3]
    block_total = pattern.shape[0]
    grid_index = lax.axis_index("grid")
    band_index = lax.axis_index("band")
    every = lax.all_gather(orbitals, "band", axis=0, tiled=True)
    local_cell = pivots - grid_index * (slab_planes * length * length)
    inside = (local_cell >= 0) & (local_cell < slab_planes * length * length)
    cell = jnp.clip(local_cell, 0, slab_planes * length * length - 1)
    rows = jnp.take(orbitals.reshape(slab_planes * length, length), cell // length, axis=0)
    lanes = jnp.arange(length, dtype=jnp.int32)
    sampled = jnp.sum(jnp.where(lanes[None, :] == (cell % length)[:, None], rows, 0.0), axis=1)
    own = jnp.where(inside, sampled, 0.0)
    ids = jnp.arange(block_total, dtype=jnp.int32)
    picked = summed(jnp.where(ids[:, None] == band_index, own[None, :], 0.0))
    gram_matrix = jnp.dot(picked.T, picked, precision=precise)
    factor = jnp.linalg.cholesky(gram_matrix)
    rotation = lax.linalg.triangular_solve(factor, picked.T, left_side=True, lower=True).T
    firsts, seconds = assignment(pattern)
    selectors = jnp.stack(
        [
            (ids == band_index).astype(jnp.float32),
            lax.dynamic_index_in_dim(firsts, band_index, 0, keepdims=False),
            lax.dynamic_index_in_dim(seconds, band_index, 0, keepdims=False),
        ]
    )
    coefficients = jnp.dot(selectors, rotation.T, precision=precise)
    depth = length // lax.axis_size("grid")
    kernel = coulomb(length, grid_index * depth, depth)
    localized, exchange_term = exchanged(coefficients, firsts, every, kernel)
    return (localized[None], exchange_term[None])


def solution(mesh):
    return jax.shard_map(
        local,
        mesh=mesh,
        in_specs=(P("band", "grid", None, None), P(), P()),
        out_specs=(P("band", "grid", None, None), P("band", "grid", None, None)),
        check_vma=False,
    )
```

```python
import functools

import jax
import jax.numpy as jnp
import numpy as np
from jax import lax
from jax.experimental import pallas as pl
from jax.experimental.pallas import tpu as pltpu
from jax.sharding import PartitionSpec as P

precise = lax.Precision.HIGHEST
MESH = pl.DeviceIdType.MESH


def complex_table(length):
    across = np.arange(length)
    angles = (across[:, None] * across[None, :] % length) * (2.0 * np.pi / length)
    cosine, sine = np.cos(angles), np.sin(angles)
    return np.block([[cosine, -sine], [sine, cosine]]).astype(np.float32)


def wrapped(indices, length):
    return jnp.where(indices < length // 2, indices, indices - length)


def coulomb(length, row_start, row_count):
    wave = wrapped(jnp.arange(length, dtype=jnp.int32), length).astype(jnp.float32)
    rows = wrapped(row_start + jnp.arange(row_count, dtype=jnp.int32), length).astype(jnp.float32)
    squared = rows[:, None, None] ** 2 + wave[None, :, None] ** 2 + wave[None, None, :] ** 2
    scaling = float(length) ** 1.5
    return jnp.where(squared > 0, 0.25 / (scaling * jnp.maximum(squared, 1.0)), 0.0)


def times(left, right):
    return jnp.dot(left, right, precision=precise, preferred_element_type=jnp.float32)


def sum_kernel(n, bands, own_ref, out_ref, wide, from_grid, from_band, sems):
    grid_me, band_me = lax.axis_index("grid"), lax.axis_index("band")
    barrier = pltpu.get_barrier_semaphore()
    axes = (("grid", n, grid_me), ("band", bands, band_me))
    for axis, count, me in axes:
        for step in range(1, count):
            pl.semaphore_signal(
                barrier, inc=1, device_id={axis: lax.rem(me + step, count)}, device_id_type=MESH
            )
    pl.semaphore_wait(barrier, n + bands - 2)
    total = own_ref[...]
    for place, (axis, count, me) in enumerate(axes):
        wide[place] = total
        landing = (from_grid, from_band)[place]
        copies = []
        for step in range(1, count):
            copy = pltpu.make_async_remote_copy(
                src_ref=wide.at[place],
                dst_ref=landing.at[step],
                send_sem=sems.at[place, 0, step],
                recv_sem=sems.at[place, 1, step],
                device_id={axis: lax.rem(me + step, count)},
                device_id_type=MESH,
            )
            copy.start()
            copies.append(copy)
        for step, copy in enumerate(copies):
            copy.wait()
            total = total + landing[step + 1]
    out_ref[...] = total


def summed(table):
    n, bands = lax.axis_size("grid"), lax.axis_size("band")
    tile = (-(-table.shape[0] // 8) * 8, 128)
    vmem = pl.BlockSpec(memory_space=pltpu.VMEM)
    padded = jnp.pad(
        table, ((0, tile[0] - table.shape[0]), (0, tile[1] - table.shape[1]))
    )
    result = pl.pallas_call(
        functools.partial(sum_kernel, n, bands),
        out_shape=jax.ShapeDtypeStruct(tile, jnp.float32),
        in_specs=[vmem],
        out_specs=vmem,
        scratch_shapes=[
            pltpu.VMEM((2,) + tile, jnp.float32),
            pltpu.VMEM((n,) + tile, jnp.float32),
            pltpu.VMEM((bands,) + tile, jnp.float32),
            pltpu.SemaphoreType.DMA((2, 2, max(n, bands))),
        ],
        compiler_params=pltpu.CompilerParams(collective_id=1, has_side_effects=True),
    )(padded)
    return result[: table.shape[0], : table.shape[1]]


def transform_kernel(
    n, halves, chunks, chips,
    mix_ref, share_ref, orbital_ref, kern_ref, fwd_ref, bwd_ref,
    own_ref, term_ref,
    send_one, recv_one, send_two, recv_two, second_ref, off_ref, twin_ref, going, coming, every_ref,
    sems_one_send, sems_one_recv, sems_two_send, sems_two_recv, sems_own, sems_twin, sems_chip, sems_in, sems_keep,
):
    bands = every_ref.shape[0]
    planes, length = own_ref.shape[0], own_ref.shape[2]
    band_me = lax.axis_index("band")
    chip, core = band_me // 2, lax.rem(band_me, 2)
    partner = chip * 2 + 1 - core
    peers = [lax.rem(chip + step, chips) * 2 + core for step in range(1, chips)]
    depth = length // n
    rows = depth // halves
    chunk = planes // chunks
    me = lax.axis_index("grid")
    barrier = pltpu.get_barrier_semaphore()
    for step in range(1, n):
        pl.semaphore_signal(
            barrier, inc=1, device_id={"grid": lax.rem(me + step, n)}, device_id_type=MESH
        )
    for peer in [partner] + peers:
        pl.semaphore_signal(barrier, inc=1, device_id={"band": peer}, device_id_type=MESH)
    pl.semaphore_wait(barrier, n - 1 + chips)

    def part_copy(source, band, part, slot, target):
        place = pl.ds(part * chunk, chunk)
        return pltpu.make_async_remote_copy(
            src_ref=source.at[place],
            dst_ref=every_ref.at[band, place],
            send_sem=sems_in.at[0, part, slot],
            recv_sem=sems_in.at[1, part, slot],
            device_id={"band": target},
            device_id_type=MESH,
        )

    def direct_copies(part):
        return [
            part_copy(orbital_ref, band_me, part, slot, target)
            for slot, target in enumerate(peers + [partner])
        ]

    def passed_copies(part):
        copies = []
        for step in range(1, chips):
            band = lax.rem(chip + chips - step, chips) * 2 + core
            copies.append(part_copy(every_ref.at[band], band, part, chips - 1 + step, partner))
        return copies

    keep = pltpu.make_async_copy(orbital_ref, every_ref.at[band_me], sems_keep.at[0])
    keep.start()
    for part in range(min(2, chunks)):
        for copy in direct_copies(part):
            copy.start()
    keep.wait()

    def out_copies(part, half):
        size = chunk * rows
        mine = pl.ds(pl.multiple_of(me * (planes * rows) + part * size, size), size)
        copies = []
        for step in range(1, n):
            target = lax.rem(me + step, n)
            copies.append(
                pltpu.make_async_remote_copy(
                    src_ref=send_one.at[target, half, :, pl.ds(part * size, size), :],
                    dst_ref=recv_one.at[half, :, mine, :],
                    send_sem=sems_one_send.at[part, half, step],
                    recv_sem=sems_one_recv.at[part, half, step],
                    device_id={"grid": target},
                    device_id_type=MESH,
                )
            )
        return copies

    def own_copy(half):
        size = planes * rows
        return pltpu.make_async_copy(
            send_one.at[me, half],
            recv_one.at[half, :, pl.ds(pl.multiple_of(me * size, size), size), :],
            sems_own.at[half],
        )

    def back_copies(half, part):
        size = planes * rows
        step_size = chunk * rows
        copies = []
        for step in range(1, n):
            target = lax.rem(me + step, n)
            start = pl.multiple_of(target * size + part * step_size, step_size)
            copies.append(
                pltpu.make_async_remote_copy(
                    src_ref=send_two.at[half, :, pl.ds(start, step_size), :],
                    dst_ref=recv_two.at[half, me, :, pl.ds(part * step_size, step_size), :],
                    send_sem=sems_two_send.at[part, half, step],
                    recv_sem=sems_two_recv.at[part, half, step],
                    device_id={"grid": target},
                    device_id_type=MESH,
                )
            )
        return copies

    def own_back(half):
        size = planes * rows
        return pltpu.make_async_copy(
            send_two.at[half, :, pl.ds(pl.multiple_of(me * size, size), size), :],
            recv_two.at[half, me],
            sems_own.at[halves + half],
        )

    def ahead(pair, carry):
        pieces = []
        for which in range(2):
            plane = pair * 2 + which
            values = [every_ref[band, plane] for band in range(bands)]
            own, first, second = [
                sum(mix_ref[kind, band] * values[band] for band in range(1, bands))
                + mix_ref[kind, 0] * values[0]
                for kind in range(3)
            ]
            own_ref[plane] = own
            second_ref[plane] = second
            both = jnp.concatenate([own * own, first * second], axis=1)
            spectrum = times(both, fwd_ref[...])
            pieces.append(
                jnp.concatenate([spectrum[:, :length], spectrum[:, length:]], axis=0)
            )
        result = times(bwd_ref[...], jnp.concatenate(pieces, axis=1))
        for which in range(2):
            for target in range(n):
                for half in range(halves):
                    for part in range(2):
                        low = part * length + target * depth + half * rows
                        send_one[target, half, part, pl.ds((pair * 2 + which) * rows, rows), :] = (
                            result[low : low + rows, which * length : (which + 1) * length]
                        )
        return carry

    for part in range(chunks):
        for copy in direct_copies(part):
            copy.wait_recv()
        for copy in passed_copies(part):
            copy.start()
        if part + 2 < chunks:
            for copy in direct_copies(part + 2):
                copy.start()
        for copy in passed_copies(part):
            copy.wait_recv()
        lax.fori_loop(part * chunk // 2, (part + 1) * chunk // 2, ahead, 0)
        for copy in out_copies(part, 0):
            copy.start()
    for half in range(1, halves):
        for part in range(chunks):
            for copy in out_copies(part, half - 1):
                copy.wait_send()
            for copy in out_copies(part, half):
                copy.start()
    for half in range(halves):
        own_copy(half).start()

    for half in range(halves):
        own_copy(half).wait()
        for part in range(chunks):
            for copy in out_copies(part, half):
                copy.wait_recv()

        def columns(pair, carry):
            pieces = []
            for which in range(2):
                place = pl.ds(pair * 2 + which, length, stride=rows)
                pieces.append(
                    jnp.concatenate(
                        [recv_one[half, 0, place, :], recv_one[half, 1, place, :]], axis=0
                    )
                )
            spectrum = times(bwd_ref[...], jnp.concatenate(pieces, axis=1))
            weights = jnp.concatenate(
                [kern_ref[half * rows + pair * 2], kern_ref[half * rows + pair * 2 + 1]], axis=1
            )
            spectrum = spectrum * jnp.concatenate([weights, weights], axis=0)
            result = times(fwd_ref[...], spectrum)
            for which in range(2):
                place = pl.ds(pair * 2 + which, length, stride=rows)
                lanes = slice(which * length, (which + 1) * length)
                send_two[half, 0, place, :] = result[:length, lanes]
                send_two[half, 1, place, :] = result[length:, lanes]
            return carry

        lax.fori_loop(0, rows // 2, columns, 0)
        own_back(half).start()
        if half < halves - 1:
            for part in range(chunks):
                for copy in back_copies(half, part):
                    copy.start()
    for half in range(halves - 1):
        for part in range(chunks):
            for copy in back_copies(half, part):
                copy.wait_send()
            if half == halves - 2 and part >= chunks - min(2, chunks):
                for copy in back_copies(halves - 1, part - chunks + min(2, chunks)):
                    copy.start()
    if halves == 1:
        for part in range(min(2, chunks)):
            for copy in back_copies(0, part):
                copy.start()

    for half in range(halves):
        own_back(half).wait()

    def twin_copy(part):
        place = pl.ds(part * chunk, chunk)
        return pltpu.make_async_remote_copy(
            src_ref=off_ref.at[place],
            dst_ref=twin_ref.at[place],
            send_sem=sems_twin.at[0, part],
            recv_sem=sems_twin.at[1, part],
            device_id={"band": partner},
            device_id_type=MESH,
        )

    def chip_copies(part):
        place = pl.ds(part * chunk, chunk)
        return [
            pltpu.make_async_remote_copy(
                src_ref=going.at[step, place],
                dst_ref=coming.at[step, place],
                send_sem=sems_chip.at[0, part, step],
                recv_sem=sems_chip.at[1, part, step],
                device_id={"band": peer},
                device_id_type=MESH,
            )
            for step, peer in enumerate(peers)
        ]

    def shared(part):
        twin_copy(part).wait_recv()

        def one(plane, carry):
            mine, other = off_ref[plane], twin_ref[plane]
            for step, peer in enumerate(peers):
                going[step, plane] = (
                    share_ref[band_me, peer] * mine + share_ref[partner, peer] * other
                )
            term_ref[plane] = (
                term_ref[plane]
                + share_ref[band_me, band_me] * mine
                + share_ref[partner, band_me] * other
            )
            return carry

        lax.fori_loop(part * chunk, (part + 1) * chunk, one, 0)
        for copy in chip_copies(part):
            copy.start()

    def home(pair, carry):
        pieces = []
        for which in range(2):
            place = pl.ds((pair * 2 + which) * rows, rows)
            pieces.append(
                jnp.concatenate(
                    [
                        recv_two[half, source, part, place, :]
                        for part in range(2)
                        for source in range(n)
                        for half in range(halves)
                    ],
                    axis=0,
                )
            )
        result = times(fwd_ref[...], jnp.concatenate(pieces, axis=1))
        for which in range(2):
            plane = pair * 2 + which
            lanes = slice(which * length, (which + 1) * length)
            both = jnp.concatenate([result[:length, lanes], result[length:, lanes]], axis=1)
            potential = times(both, bwd_ref[...])
            term_ref[plane] = potential[:, :length] * own_ref[plane]
            off_ref[plane] = potential[:, length:] * second_ref[plane]
        return carry

    for part in range(chunks):
        for copy in back_copies(halves - 1, part):
            copy.wait_send()
        if part + 2 < chunks:
            for copy in back_copies(halves - 1, part + 2):
                copy.start()
        for half in range(halves):
            for copy in back_copies(half, part):
                copy.wait_recv()
        lax.fori_loop(part * chunk // 2, (part + 1) * chunk // 2, home, 0)
        twin_copy(part).start()
        if part > 0:
            shared(part - 1)
    shared(chunks - 1)

    def last(plane, carry):
        total = term_ref[plane]
        for step in range(chips - 1):
            total = total + coming[step, plane]
        term_ref[plane] = total
        return carry

    for part in range(chunks):
        for copy in chip_copies(part):
            copy.wait()
        lax.fori_loop(part * chunk, (part + 1) * chunk, last, 0)
        twin_copy(part).wait_send()
    for part in range(chunks):
        for copy in out_copies(part, halves - 1):
            copy.wait_send()
        for copy in direct_copies(part) + passed_copies(part):
            copy.wait_send()


def exchanged(mix, share, orbital, kernel):
    n = lax.axis_size("grid")
    planes, length = orbital.shape[0], orbital.shape[2]
    chips = lax.axis_size("band") // 2
    depth = length // n
    halves = 2 if depth % 16 == 0 else 1
    rows = depth // halves
    chunk = max(planes // 4, 2)
    chunks = planes // chunk
    forward = complex_table(length)
    vmem = pl.BlockSpec(memory_space=pltpu.VMEM)
    smem = pl.BlockSpec(memory_space=pltpu.SMEM)
    slab = jax.ShapeDtypeStruct(orbital.shape, jnp.float32)
    block = planes * rows
    return pl.pallas_call(
        functools.partial(transform_kernel, n, halves, chunks, chips),
        out_shape=(slab, slab),
        in_specs=[smem] * 2 + [vmem] * 4,
        out_specs=(vmem, vmem),
        scratch_shapes=[
            pltpu.VMEM((n, halves, 2, block, length), jnp.float32),
            pltpu.VMEM((halves, 2, n * block, length), jnp.float32),
            pltpu.VMEM((halves, 2, n * block, length), jnp.float32),
            pltpu.VMEM((halves, n, 2, block, length), jnp.float32),
            pltpu.VMEM(slab.shape, jnp.float32),
            pltpu.VMEM(slab.shape, jnp.float32),
            pltpu.VMEM(slab.shape, jnp.float32),
            pltpu.VMEM((chips - 1,) + slab.shape, jnp.float32),
            pltpu.VMEM((chips - 1,) + slab.shape, jnp.float32),
            pltpu.VMEM((2 * chips,) + slab.shape, jnp.float32),
            pltpu.SemaphoreType.DMA((chunks, halves, n)),
            pltpu.SemaphoreType.DMA((chunks, halves, n)),
            pltpu.SemaphoreType.DMA((chunks, halves, n)),
            pltpu.SemaphoreType.DMA((chunks, halves, n)),
            pltpu.SemaphoreType.DMA((2 * halves,)),
            pltpu.SemaphoreType.DMA((2, chunks)),
            pltpu.SemaphoreType.DMA((2, chunks, max(chips - 1, 1))),
            pltpu.SemaphoreType.DMA((2, chunks, 2 * chips - 1)),
            pltpu.SemaphoreType.DMA((1,)),
        ],
        compiler_params=pltpu.CompilerParams(
            collective_id=0, has_side_effects=True, vmem_limit_bytes=40 * 1024 * 1024
        ),
    )(mix, share, orbital, kernel, jnp.asarray(forward), jnp.asarray(forward.T.copy()))


def assignment(pattern):
    blocks = pattern.shape[0]
    ids = jnp.arange(blocks, dtype=jnp.int32)
    off = ((pattern == 1) & (ids[:, None] != ids[None, :])).astype(jnp.int32).reshape(-1)
    before = jnp.cumsum(off) - off
    chosen = (off[None, :] == 1) & (before[None, :] == ids[:, None])
    chosen = chosen.reshape(blocks, blocks, blocks)
    firsts = jnp.any(chosen, axis=2).astype(jnp.float32)
    seconds = jnp.any(chosen, axis=1).astype(jnp.float32)
    return firsts, seconds


def local(orbitals, pivots, pattern):
    slab_planes = orbitals.shape[1]
    length = orbitals.shape[3]
    block_total = pattern.shape[0]
    grid_index = lax.axis_index("grid")
    band_index = lax.axis_index("band")
    local_cell = pivots - grid_index * (slab_planes * length * length)
    inside = (local_cell >= 0) & (local_cell < slab_planes * length * length)
    cell = jnp.clip(local_cell, 0, slab_planes * length * length - 1)
    rows = jnp.take(orbitals.reshape(slab_planes * length, length), cell // length, axis=0)
    lanes = jnp.arange(length, dtype=jnp.int32)
    sampled = jnp.sum(jnp.where(lanes[None, :] == (cell % length)[:, None], rows, 0.0), axis=1)
    own = jnp.where(inside, sampled, 0.0)
    ids = jnp.arange(block_total, dtype=jnp.int32)
    picked = summed(jnp.where(ids[:, None] == band_index, own[None, :], 0.0))
    gram_matrix = jnp.dot(picked.T, picked, precision=precise)
    factor = jnp.linalg.cholesky(gram_matrix)
    rotation = lax.linalg.triangular_solve(factor, picked.T, left_side=True, lower=True).T
    firsts, seconds = assignment(pattern)
    selectors = jnp.stack(
        [
            (ids == band_index).astype(jnp.float32),
            lax.dynamic_index_in_dim(firsts, band_index, 0, keepdims=False),
            lax.dynamic_index_in_dim(seconds, band_index, 0, keepdims=False),
        ]
    )
    coefficients = jnp.dot(selectors, rotation.T, precision=precise)
    depth = length // lax.axis_size("grid")
    kernel = coulomb(length, grid_index * depth, depth)
    localized, exchange_term = exchanged(coefficients, firsts, orbitals[0], kernel)
    return (localized[None], exchange_term[None])


def solution(mesh):
    return jax.shard_map(
        local,
        mesh=mesh,
        in_specs=(P("band", "grid", None, None), P(), P()),
        out_specs=(P("band", "grid", None, None), P("band", "grid", None, None)),
        check_vma=False,
    )
```

```python
import functools

import jax
import jax.numpy as jnp
import numpy as np
from jax import lax
from jax.experimental import pallas as pl
from jax.experimental.pallas import tpu as pltpu
from jax.sharding import PartitionSpec as P

precise = lax.Precision.HIGHEST
MESH = pl.DeviceIdType.MESH


def complex_table(length):
    across = np.arange(length)
    angles = (across[:, None] * across[None, :] % length) * (2.0 * np.pi / length)
    cosine, sine = np.cos(angles), np.sin(angles)
    return np.block([[cosine, -sine], [sine, cosine]]).astype(np.float32)


def wrapped(indices, length):
    return jnp.where(indices < length // 2, indices, indices - length)


def coulomb(length, row_start, row_count):
    wave = wrapped(jnp.arange(length, dtype=jnp.int32), length).astype(jnp.float32)
    rows = wrapped(row_start + jnp.arange(row_count, dtype=jnp.int32), length).astype(jnp.float32)
    squared = rows[:, None, None] ** 2 + wave[None, :, None] ** 2 + wave[None, None, :] ** 2
    scaling = float(length) ** 1.5
    return jnp.where(squared > 0, 0.25 / (scaling * jnp.maximum(squared, 1.0)), 0.0)


def times(left, right):
    return jnp.dot(left, right, precision=precise, preferred_element_type=jnp.float32)


def sum_kernel(n, bands, own_ref, out_ref, wide, from_grid, from_band, sems):
    grid_me, band_me = lax.axis_index("grid"), lax.axis_index("band")
    barrier = pltpu.get_barrier_semaphore()
    axes = (("grid", n, grid_me), ("band", bands, band_me))
    for axis, count, me in axes:
        for step in range(1, count):
            pl.semaphore_signal(
                barrier, inc=1, device_id={axis: lax.rem(me + step, count)}, device_id_type=MESH
            )
    pl.semaphore_wait(barrier, n + bands - 2)
    total = own_ref[...]
    for place, (axis, count, me) in enumerate(axes):
        wide[place] = total
        landing = (from_grid, from_band)[place]
        copies = []
        for step in range(1, count):
            copy = pltpu.make_async_remote_copy(
                src_ref=wide.at[place],
                dst_ref=landing.at[step],
                send_sem=sems.at[place, 0, step],
                recv_sem=sems.at[place, 1, step],
                device_id={axis: lax.rem(me + step, count)},
                device_id_type=MESH,
            )
            copy.start()
            copies.append(copy)
        for step, copy in enumerate(copies):
            copy.wait()
            total = total + landing[step + 1]
    out_ref[...] = total


def summed(table):
    n, bands = lax.axis_size("grid"), lax.axis_size("band")
    tile = (-(-table.shape[0] // 8) * 8, 128)
    vmem = pl.BlockSpec(memory_space=pltpu.VMEM)
    padded = jnp.pad(
        table, ((0, tile[0] - table.shape[0]), (0, tile[1] - table.shape[1]))
    )
    result = pl.pallas_call(
        functools.partial(sum_kernel, n, bands),
        out_shape=jax.ShapeDtypeStruct(tile, jnp.float32),
        in_specs=[vmem],
        out_specs=vmem,
        scratch_shapes=[
            pltpu.VMEM((2,) + tile, jnp.float32),
            pltpu.VMEM((n,) + tile, jnp.float32),
            pltpu.VMEM((bands,) + tile, jnp.float32),
            pltpu.SemaphoreType.DMA((2, 2, max(n, bands))),
        ],
        compiler_params=pltpu.CompilerParams(collective_id=1, has_side_effects=True),
    )(padded)
    return result[: table.shape[0], : table.shape[1]]


def transform_kernel(
    n, halves, chunks, chips,
    mix_ref, share_ref, orbital_ref, kern_ref, fwd_ref, bwd_ref,
    own_ref, term_ref,
    send_one, recv_one, send_two, recv_two, second_ref, off_ref, twin_ref, going, coming, every_ref,
    sems_one_send, sems_one_recv, sems_two_send, sems_two_recv, sems_own, sems_twin, sems_chip, sems_in, sems_keep,
):
    bands = every_ref.shape[0]
    planes, length = own_ref.shape[0], own_ref.shape[2]
    band_me = lax.axis_index("band")
    chip, core = band_me // 2, lax.rem(band_me, 2)
    partner = chip * 2 + 1 - core
    peers = [lax.rem(chip + step, chips) * 2 + core for step in range(1, chips)]
    depth = length // n
    rows = depth // halves
    chunk = planes // chunks
    me = lax.axis_index("grid")
    barrier = pltpu.get_barrier_semaphore()
    for step in range(1, n):
        pl.semaphore_signal(
            barrier, inc=1, device_id={"grid": lax.rem(me + step, n)}, device_id_type=MESH
        )
    for peer in [partner] + peers:
        pl.semaphore_signal(barrier, inc=1, device_id={"band": peer}, device_id_type=MESH)
    pl.semaphore_wait(barrier, n - 1 + chips)

    def part_copy(source, band, part, slot, target):
        place = pl.ds(part * chunk, chunk)
        return pltpu.make_async_remote_copy(
            src_ref=source.at[place],
            dst_ref=every_ref.at[band, place],
            send_sem=sems_in.at[0, part, slot],
            recv_sem=sems_in.at[1, part, slot],
            device_id={"band": target},
            device_id_type=MESH,
        )

    def direct_copies(part):
        return [
            part_copy(orbital_ref, band_me, part, slot, target)
            for slot, target in enumerate(peers + [partner])
        ]

    def passed_copies(part):
        copies = []
        for step in range(1, chips):
            band = lax.rem(chip + chips - step, chips) * 2 + core
            copies.append(part_copy(every_ref.at[band], band, part, chips - 1 + step, partner))
        return copies

    keep = pltpu.make_async_copy(orbital_ref, every_ref.at[band_me], sems_keep.at[0])
    keep.start()
    for part in range(min(2, chunks)):
        for copy in direct_copies(part):
            copy.start()
    keep.wait()

    farthest = sorted(range(1, n), key=lambda step: (-min(step, n - step), step))

    def out_copies(part, half):
        size = chunk * rows
        mine = pl.ds(pl.multiple_of(me * (planes * rows) + part * size, size), size)
        copies = []
        for step in farthest:
            target = lax.rem(me + step, n)
            copies.append(
                pltpu.make_async_remote_copy(
                    src_ref=send_one.at[target, half, :, pl.ds(part * size, size), :],
                    dst_ref=recv_one.at[half, :, mine, :],
                    send_sem=sems_one_send.at[part, half, step],
                    recv_sem=sems_one_recv.at[part, half, step],
                    device_id={"grid": target},
                    device_id_type=MESH,
                )
            )
        return copies

    def own_copy(half):
        size = planes * rows
        return pltpu.make_async_copy(
            send_one.at[me, half],
            recv_one.at[half, :, pl.ds(pl.multiple_of(me * size, size), size), :],
            sems_own.at[half],
        )

    def back_copies(half, part):
        size = planes * rows
        step_size = chunk * rows
        copies = []
        for step in farthest:
            target = lax.rem(me + step, n)
            start = pl.multiple_of(target * size + part * step_size, step_size)
            copies.append(
                pltpu.make_async_remote_copy(
                    src_ref=send_two.at[half, :, pl.ds(start, step_size), :],
                    dst_ref=recv_two.at[half, me, :, pl.ds(part * step_size, step_size), :],
                    send_sem=sems_two_send.at[part, half, step],
                    recv_sem=sems_two_recv.at[part, half, step],
                    device_id={"grid": target},
                    device_id_type=MESH,
                )
            )
        return copies

    def own_back(half):
        size = planes * rows
        return pltpu.make_async_copy(
            send_two.at[half, :, pl.ds(pl.multiple_of(me * size, size), size), :],
            recv_two.at[half, me],
            sems_own.at[halves + half],
        )

    def ahead(pair, carry):
        pieces = []
        for which in range(2):
            plane = pair * 2 + which
            values = [every_ref[band, plane] for band in range(bands)]
            own, first, second = [
                sum(mix_ref[kind, band] * values[band] for band in range(1, bands))
                + mix_ref[kind, 0] * values[0]
                for kind in range(3)
            ]
            own_ref[plane] = own
            second_ref[plane] = second
            both = jnp.concatenate([own * own, first * second], axis=1)
            spectrum = times(both, fwd_ref[...])
            pieces.append(
                jnp.concatenate([spectrum[:, :length], spectrum[:, length:]], axis=0)
            )
        result = times(bwd_ref[...], jnp.concatenate(pieces, axis=1))
        for which in range(2):
            for target in range(n):
                for half in range(halves):
                    for part in range(2):
                        low = part * length + target * depth + half * rows
                        send_one[target, half, part, pl.ds((pair * 2 + which) * rows, rows), :] = (
                            result[low : low + rows, which * length : (which + 1) * length]
                        )
        return carry

    for part in range(chunks):
        for copy in direct_copies(part):
            copy.wait_recv()
        for copy in passed_copies(part):
            copy.start()
        if part + 2 < chunks:
            for copy in direct_copies(part + 2):
                copy.start()
        for copy in passed_copies(part):
            copy.wait_recv()
        lax.fori_loop(part * chunk // 2, (part + 1) * chunk // 2, ahead, 0)
        for copy in out_copies(part, 0):
            copy.start()
    for half in range(1, halves):
        for part in range(chunks):
            for copy in out_copies(part, half - 1):
                copy.wait_send()
            for copy in out_copies(part, half):
                copy.start()
    for half in range(halves):
        own_copy(half).start()

    for half in range(halves):
        own_copy(half).wait()
        for part in range(chunks):
            for copy in out_copies(part, half):
                copy.wait_recv()

        def columns(pair, carry):
            pieces = []
            for which in range(2):
                place = pl.ds(pair * 2 + which, length, stride=rows)
                pieces.append(
                    jnp.concatenate(
                        [recv_one[half, 0, place, :], recv_one[half, 1, place, :]], axis=0
                    )
                )
            spectrum = times(bwd_ref[...], jnp.concatenate(pieces, axis=1))
            weights = jnp.concatenate(
                [kern_ref[half * rows + pair * 2], kern_ref[half * rows + pair * 2 + 1]], axis=1
            )
            spectrum = spectrum * jnp.concatenate([weights, weights], axis=0)
            result = times(fwd_ref[...], spectrum)
            for which in range(2):
                place = pl.ds(pair * 2 + which, length, stride=rows)
                lanes = slice(which * length, (which + 1) * length)
                send_two[half, 0, place, :] = result[:length, lanes]
                send_two[half, 1, place, :] = result[length:, lanes]
            return carry

        lax.fori_loop(0, rows // 2, columns, 0)
        own_back(half).start()
        if half < halves - 1:
            for part in range(chunks):
                for copy in back_copies(half, part):
                    copy.start()
    for half in range(halves - 1):
        for part in range(chunks):
            for copy in back_copies(half, part):
                copy.wait_send()
            if half == halves - 2 and part >= chunks - min(2, chunks):
                for copy in back_copies(halves - 1, part - chunks + min(2, chunks)):
                    copy.start()
    if halves == 1:
        for part in range(min(2, chunks)):
            for copy in back_copies(0, part):
                copy.start()

    for half in range(halves):
        own_back(half).wait()

    def twin_copy(part):
        place = pl.ds(part * chunk, chunk)
        return pltpu.make_async_remote_copy(
            src_ref=off_ref.at[place],
            dst_ref=twin_ref.at[place],
            send_sem=sems_twin.at[0, part],
            recv_sem=sems_twin.at[1, part],
            device_id={"band": partner},
            device_id_type=MESH,
        )

    def chip_copies(part):
        place = pl.ds(part * chunk, chunk)
        return [
            pltpu.make_async_remote_copy(
                src_ref=going.at[step, place],
                dst_ref=coming.at[step, place],
                send_sem=sems_chip.at[0, part, step],
                recv_sem=sems_chip.at[1, part, step],
                device_id={"band": peer},
                device_id_type=MESH,
            )
            for step, peer in enumerate(peers)
        ]

    def shared(part):
        twin_copy(part).wait_recv()

        def one(plane, carry):
            mine, other = off_ref[plane], twin_ref[plane]
            for step, peer in enumerate(peers):
                going[step, plane] = (
                    share_ref[band_me, peer] * mine + share_ref[partner, peer] * other
                )
            term_ref[plane] = (
                term_ref[plane]
                + share_ref[band_me, band_me] * mine
                + share_ref[partner, band_me] * other
            )
            return carry

        lax.fori_loop(part * chunk, (part + 1) * chunk, one, 0)
        for copy in chip_copies(part):
            copy.start()

    def home(pair, carry):
        pieces = []
        for which in range(2):
            place = pl.ds((pair * 2 + which) * rows, rows)
            pieces.append(
                jnp.concatenate(
                    [
                        recv_two[half, source, part, place, :]
                        for part in range(2)
                        for source in range(n)
                        for half in range(halves)
                    ],
                    axis=0,
                )
            )
        result = times(fwd_ref[...], jnp.concatenate(pieces, axis=1))
        for which in range(2):
            plane = pair * 2 + which
            lanes = slice(which * length, (which + 1) * length)
            both = jnp.concatenate([result[:length, lanes], result[length:, lanes]], axis=1)
            potential = times(both, bwd_ref[...])
            term_ref[plane] = potential[:, :length] * own_ref[plane]
            off_ref[plane] = potential[:, length:] * second_ref[plane]
        return carry

    for part in range(chunks):
        for copy in back_copies(halves - 1, part):
            copy.wait_send()
        if part + 2 < chunks:
            for copy in back_copies(halves - 1, part + 2):
                copy.start()
        for half in range(halves):
            for copy in back_copies(half, part):
                copy.wait_recv()
        lax.fori_loop(part * chunk // 2, (part + 1) * chunk // 2, home, 0)
        twin_copy(part).start()
        if part > 0:
            shared(part - 1)
    shared(chunks - 1)

    def last(plane, carry):
        total = term_ref[plane]
        for step in range(chips - 1):
            total = total + coming[step, plane]
        term_ref[plane] = total
        return carry

    for part in range(chunks):
        for copy in chip_copies(part):
            copy.wait()
        lax.fori_loop(part * chunk, (part + 1) * chunk, last, 0)
        twin_copy(part).wait_send()
    for part in range(chunks):
        for copy in out_copies(part, halves - 1):
            copy.wait_send()
        for copy in direct_copies(part) + passed_copies(part):
            copy.wait_send()


def exchanged(mix, share, orbital, kernel):
    n = lax.axis_size("grid")
    planes, length = orbital.shape[0], orbital.shape[2]
    chips = lax.axis_size("band") // 2
    depth = length // n
    halves = 2 if depth % 16 == 0 else 1
    rows = depth // halves
    chunk = max(planes // 4, 2)
    chunks = planes // chunk
    forward = complex_table(length)
    vmem = pl.BlockSpec(memory_space=pltpu.VMEM)
    smem = pl.BlockSpec(memory_space=pltpu.SMEM)
    slab = jax.ShapeDtypeStruct(orbital.shape, jnp.float32)
    block = planes * rows
    return pl.pallas_call(
        functools.partial(transform_kernel, n, halves, chunks, chips),
        out_shape=(slab, slab),
        in_specs=[smem] * 2 + [vmem] * 4,
        out_specs=(vmem, vmem),
        scratch_shapes=[
            pltpu.VMEM((n, halves, 2, block, length), jnp.float32),
            pltpu.VMEM((halves, 2, n * block, length), jnp.float32),
            pltpu.VMEM((halves, 2, n * block, length), jnp.float32),
            pltpu.VMEM((halves, n, 2, block, length), jnp.float32),
            pltpu.VMEM(slab.shape, jnp.float32),
            pltpu.VMEM(slab.shape, jnp.float32),
            pltpu.VMEM(slab.shape, jnp.float32),
            pltpu.VMEM((chips - 1,) + slab.shape, jnp.float32),
            pltpu.VMEM((chips - 1,) + slab.shape, jnp.float32),
            pltpu.VMEM((2 * chips,) + slab.shape, jnp.float32),
            pltpu.SemaphoreType.DMA((chunks, halves, n)),
            pltpu.SemaphoreType.DMA((chunks, halves, n)),
            pltpu.SemaphoreType.DMA((chunks, halves, n)),
            pltpu.SemaphoreType.DMA((chunks, halves, n)),
            pltpu.SemaphoreType.DMA((2 * halves,)),
            pltpu.SemaphoreType.DMA((2, chunks)),
            pltpu.SemaphoreType.DMA((2, chunks, max(chips - 1, 1))),
            pltpu.SemaphoreType.DMA((2, chunks, 2 * chips - 1)),
            pltpu.SemaphoreType.DMA((1,)),
        ],
        compiler_params=pltpu.CompilerParams(
            collective_id=0, has_side_effects=True, vmem_limit_bytes=40 * 1024 * 1024
        ),
    )(mix, share, orbital, kernel, jnp.asarray(forward), jnp.asarray(forward.T.copy()))


def assignment(pattern):
    blocks = pattern.shape[0]
    ids = jnp.arange(blocks, dtype=jnp.int32)
    off = ((pattern == 1) & (ids[:, None] != ids[None, :])).astype(jnp.int32).reshape(-1)
    before = jnp.cumsum(off) - off
    chosen = (off[None, :] == 1) & (before[None, :] == ids[:, None])
    chosen = chosen.reshape(blocks, blocks, blocks)
    firsts = jnp.any(chosen, axis=2).astype(jnp.float32)
    seconds = jnp.any(chosen, axis=1).astype(jnp.float32)
    return firsts, seconds


def local(orbitals, pivots, pattern):
    slab_planes = orbitals.shape[1]
    length = orbitals.shape[3]
    block_total = pattern.shape[0]
    grid_index = lax.axis_index("grid")
    band_index = lax.axis_index("band")
    local_cell = pivots - grid_index * (slab_planes * length * length)
    inside = (local_cell >= 0) & (local_cell < slab_planes * length * length)
    cell = jnp.clip(local_cell, 0, slab_planes * length * length - 1)
    rows = jnp.take(orbitals.reshape(slab_planes * length, length), cell // length, axis=0)
    lanes = jnp.arange(length, dtype=jnp.int32)
    sampled = jnp.sum(jnp.where(lanes[None, :] == (cell % length)[:, None], rows, 0.0), axis=1)
    own = jnp.where(inside, sampled, 0.0)
    ids = jnp.arange(block_total, dtype=jnp.int32)
    picked = summed(jnp.where(ids[:, None] == band_index, own[None, :], 0.0))
    gram_matrix = jnp.dot(picked.T, picked, precision=precise)
    factor = jnp.linalg.cholesky(gram_matrix)
    rotation = lax.linalg.triangular_solve(factor, picked.T, left_side=True, lower=True).T
    firsts, seconds = assignment(pattern)
    selectors = jnp.stack(
        [
            (ids == band_index).astype(jnp.float32),
            lax.dynamic_index_in_dim(firsts, band_index, 0, keepdims=False),
            lax.dynamic_index_in_dim(seconds, band_index, 0, keepdims=False),
        ]
    )
    coefficients = jnp.dot(selectors, rotation.T, precision=precise)
    depth = length // lax.axis_size("grid")
    kernel = coulomb(length, grid_index * depth, depth)
    localized, exchange_term = exchanged(coefficients, firsts, orbitals[0], kernel)
    return (localized[None], exchange_term[None])


def solution(mesh):
    return jax.shard_map(
        local,
        mesh=mesh,
        in_specs=(P("band", "grid", None, None), P(), P()),
        out_specs=(P("band", "grid", None, None), P("band", "grid", None, None)),
        check_vma=False,
    )
```

```python
import functools

import jax
import jax.numpy as jnp
import numpy as np
from jax import lax
from jax.experimental import pallas as pl
from jax.experimental.pallas import tpu as pltpu
from jax.sharding import PartitionSpec as P

precise = lax.Precision.HIGHEST
MESH = pl.DeviceIdType.MESH


def complex_table(length):
    across = np.arange(length)
    angles = (across[:, None] * across[None, :] % length) * (2.0 * np.pi / length)
    cosine, sine = np.cos(angles), np.sin(angles)
    return np.block([[cosine, -sine], [sine, cosine]]).astype(np.float32)


def wrapped(indices, length):
    return jnp.where(indices < length // 2, indices, indices - length)


def coulomb(length, row_start, row_count):
    wave = wrapped(jnp.arange(length, dtype=jnp.int32), length).astype(jnp.float32)
    rows = wrapped(row_start + jnp.arange(row_count, dtype=jnp.int32), length).astype(jnp.float32)
    squared = rows[:, None, None] ** 2 + wave[None, :, None] ** 2 + wave[None, None, :] ** 2
    scaling = float(length) ** 1.5
    return jnp.where(squared > 0, 0.25 / (scaling * jnp.maximum(squared, 1.0)), 0.0)


def times(left, right):
    return jnp.dot(left, right, precision=precise, preferred_element_type=jnp.float32)


def sum_kernel(n, bands, own_ref, out_ref, wide, from_grid, from_band, sems):
    grid_me, band_me = lax.axis_index("grid"), lax.axis_index("band")
    barrier = pltpu.get_barrier_semaphore()
    axes = (("grid", n, grid_me), ("band", bands, band_me))
    for axis, count, me in axes:
        for step in range(1, count):
            pl.semaphore_signal(
                barrier, inc=1, device_id={axis: lax.rem(me + step, count)}, device_id_type=MESH
            )
    pl.semaphore_wait(barrier, n + bands - 2)
    total = own_ref[...]
    for place, (axis, count, me) in enumerate(axes):
        wide[place] = total
        landing = (from_grid, from_band)[place]
        copies = []
        for step in range(1, count):
            copy = pltpu.make_async_remote_copy(
                src_ref=wide.at[place],
                dst_ref=landing.at[step],
                send_sem=sems.at[place, 0, step],
                recv_sem=sems.at[place, 1, step],
                device_id={axis: lax.rem(me + step, count)},
                device_id_type=MESH,
            )
            copy.start()
            copies.append(copy)
        for step, copy in enumerate(copies):
            copy.wait()
            total = total + landing[step + 1]
    out_ref[...] = total


def summed(table):
    n, bands = lax.axis_size("grid"), lax.axis_size("band")
    tile = (-(-table.shape[0] // 8) * 8, 128)
    vmem = pl.BlockSpec(memory_space=pltpu.VMEM)
    padded = jnp.pad(
        table, ((0, tile[0] - table.shape[0]), (0, tile[1] - table.shape[1]))
    )
    result = pl.pallas_call(
        functools.partial(sum_kernel, n, bands),
        out_shape=jax.ShapeDtypeStruct(tile, jnp.float32),
        in_specs=[vmem],
        out_specs=vmem,
        scratch_shapes=[
            pltpu.VMEM((2,) + tile, jnp.float32),
            pltpu.VMEM((n,) + tile, jnp.float32),
            pltpu.VMEM((bands,) + tile, jnp.float32),
            pltpu.SemaphoreType.DMA((2, 2, max(n, bands))),
        ],
        compiler_params=pltpu.CompilerParams(collective_id=1, has_side_effects=True),
    )(padded)
    return result[: table.shape[0], : table.shape[1]]


def transform_kernel(
    n, halves, chunks, chips,
    mix_ref, share_ref, orbital_ref, kern_ref, fwd_ref, bwd_ref,
    own_ref, term_ref,
    send_one, recv_one, send_two, recv_two, second_ref, off_ref, twin_ref, going, coming, every_ref,
    sems_one_send, sems_one_recv, sems_two_send, sems_two_recv, sems_own, sems_twin, sems_chip, sems_in, sems_keep,
):
    bands = every_ref.shape[0]
    planes, length = own_ref.shape[0], own_ref.shape[2]
    band_me = lax.axis_index("band")
    chip, core = band_me // 2, lax.rem(band_me, 2)
    partner = chip * 2 + 1 - core
    peers = [lax.rem(chip + step, chips) * 2 + core for step in range(1, chips)]
    depth = length // n
    rows = depth // halves
    chunk = planes // chunks
    me = lax.axis_index("grid")
    barrier = pltpu.get_barrier_semaphore()
    for step in range(1, n):
        pl.semaphore_signal(
            barrier, inc=1, device_id={"grid": lax.rem(me + step, n)}, device_id_type=MESH
        )
    for peer in [partner] + peers:
        pl.semaphore_signal(barrier, inc=1, device_id={"band": peer}, device_id_type=MESH)
    pl.semaphore_wait(barrier, n - 1 + chips)

    def part_copy(source, band, part, slot, target):
        place = pl.ds(part * chunk, chunk)
        return pltpu.make_async_remote_copy(
            src_ref=source.at[place],
            dst_ref=every_ref.at[band, place],
            send_sem=sems_in.at[0, part, slot],
            recv_sem=sems_in.at[1, part, slot],
            device_id={"band": target},
            device_id_type=MESH,
        )

    def direct_copies(part):
        return [
            part_copy(orbital_ref, band_me, part, slot, target)
            for slot, target in enumerate(peers + [partner])
        ]

    def passed_copies(part):
        copies = []
        for step in range(1, chips):
            band = lax.rem(chip + chips - step, chips) * 2 + core
            copies.append(part_copy(every_ref.at[band], band, part, chips - 1 + step, partner))
        return copies

    keep = pltpu.make_async_copy(orbital_ref, every_ref.at[band_me], sems_keep.at[0])
    keep.start()
    for part in range(min(2, chunks)):
        for copy in direct_copies(part):
            copy.start()
    keep.wait()

    def out_copies(part, half):
        size = chunk * rows
        mine = pl.ds(pl.multiple_of(me * (planes * rows) + part * size, size), size)
        copies = []
        for step in range(1, n):
            target = lax.rem(me + step, n)
            copies.append(
                pltpu.make_async_remote_copy(
                    src_ref=send_one.at[target, half, :, pl.ds(part * size, size), :],
                    dst_ref=recv_one.at[half, :, mine, :],
                    send_sem=sems_one_send.at[part, half, step],
                    recv_sem=sems_one_recv.at[part, half, step],
                    device_id={"grid": target},
                    device_id_type=MESH,
                )
            )
        return copies

    def own_copy(half):
        size = planes * rows
        return pltpu.make_async_copy(
            send_one.at[me, half],
            recv_one.at[half, :, pl.ds(pl.multiple_of(me * size, size), size), :],
            sems_own.at[half],
        )

    def back_copies(half, part):
        size = planes * rows
        step_size = chunk * rows
        copies = []
        for step in range(1, n):
            target = lax.rem(me + step, n)
            start = pl.multiple_of(target * size + part * step_size, step_size)
            copies.append(
                pltpu.make_async_remote_copy(
                    src_ref=send_two.at[half, :, pl.ds(start, step_size), :],
                    dst_ref=recv_two.at[half, me, :, pl.ds(part * step_size, step_size), :],
                    send_sem=sems_two_send.at[part, half, step],
                    recv_sem=sems_two_recv.at[part, half, step],
                    device_id={"grid": target},
                    device_id_type=MESH,
                )
            )
        return copies

    def own_back(half):
        size = planes * rows
        return pltpu.make_async_copy(
            send_two.at[half, :, pl.ds(pl.multiple_of(me * size, size), size), :],
            recv_two.at[half, me],
            sems_own.at[halves + half],
        )

    def ahead(pair, carry):
        pieces = []
        for which in range(2):
            plane = pair * 2 + which
            values = [every_ref[band, plane] for band in range(bands)]
            own, first, second = [
                sum(mix_ref[kind, band] * values[band] for band in range(1, bands))
                + mix_ref[kind, 0] * values[0]
                for kind in range(3)
            ]
            own_ref[plane] = own
            second_ref[plane] = second
            both = jnp.concatenate([own * own, first * second], axis=1)
            spectrum = times(both, fwd_ref[...])
            pieces.append(
                jnp.concatenate([spectrum[:, :length], spectrum[:, length:]], axis=0)
            )
        result = times(bwd_ref[...], jnp.concatenate(pieces, axis=1))
        for which in range(2):
            for target in range(n):
                for half in range(halves):
                    for part in range(2):
                        low = part * length + target * depth + half * rows
                        send_one[target, half, part, pl.ds((pair * 2 + which) * rows, rows), :] = (
                            result[low : low + rows, which * length : (which + 1) * length]
                        )
        return carry

    for part in range(chunks):
        for copy in direct_copies(part):
            copy.wait_recv()
        for copy in passed_copies(part):
            copy.start()
        if part + 2 < chunks:
            for copy in direct_copies(part + 2):
                copy.start()
        for copy in passed_copies(part):
            copy.wait_recv()
        lax.fori_loop(part * chunk // 2, (part + 1) * chunk // 2, ahead, 0)
        for copy in out_copies(part, 0):
            copy.start()
    for half in range(1, halves):
        for part in range(chunks):
            for copy in out_copies(part, half - 1):
                copy.wait_send()
            for copy in out_copies(part, half):
                copy.start()
    for half in range(halves):
        own_copy(half).start()

    for half in range(halves):
        own_copy(half).wait()
        for part in range(chunks):
            for copy in out_copies(part, half):
                copy.wait_recv()

        def columns(pair, carry):
            pieces = []
            for which in range(2):
                place = pl.ds(pair * 2 + which, length, stride=rows)
                pieces.append(
                    jnp.concatenate(
                        [recv_one[half, 0, place, :], recv_one[half, 1, place, :]], axis=0
                    )
                )
            spectrum = times(bwd_ref[...], jnp.concatenate(pieces, axis=1))
            weights = jnp.concatenate(
                [kern_ref[half * rows + pair * 2], kern_ref[half * rows + pair * 2 + 1]], axis=1
            )
            spectrum = spectrum * jnp.concatenate([weights, weights], axis=0)
            result = times(fwd_ref[...], spectrum)
            for which in range(2):
                place = pl.ds(pair * 2 + which, length, stride=rows)
                lanes = slice(which * length, (which + 1) * length)
                send_two[half, 0, place, :] = result[:length, lanes]
                send_two[half, 1, place, :] = result[length:, lanes]
            return carry

        lax.fori_loop(0, rows // 2, columns, 0)
        own_back(half).start()
        if half < halves - 1:
            for part in range(chunks):
                for copy in back_copies(half, part):
                    copy.start()
    for half in range(halves - 1):
        for part in range(chunks):
            for copy in back_copies(half, part):
                copy.wait_send()
            if half == halves - 2 and part >= chunks - min(3, chunks):
                for copy in back_copies(halves - 1, part - chunks + min(3, chunks)):
                    copy.start()
    if halves == 1:
        for part in range(min(3, chunks)):
            for copy in back_copies(0, part):
                copy.start()

    for half in range(halves):
        own_back(half).wait()

    def twin_copy(part):
        place = pl.ds(part * chunk, chunk)
        return pltpu.make_async_remote_copy(
            src_ref=off_ref.at[place],
            dst_ref=twin_ref.at[place],
            send_sem=sems_twin.at[0, part],
            recv_sem=sems_twin.at[1, part],
            device_id={"band": partner},
            device_id_type=MESH,
        )

    def chip_copies(part):
        place = pl.ds(part * chunk, chunk)
        return [
            pltpu.make_async_remote_copy(
                src_ref=going.at[step, place],
                dst_ref=coming.at[step, place],
                send_sem=sems_chip.at[0, part, step],
                recv_sem=sems_chip.at[1, part, step],
                device_id={"band": peer},
                device_id_type=MESH,
            )
            for step, peer in enumerate(peers)
        ]

    def shared(part):
        twin_copy(part).wait_recv()

        def one(plane, carry):
            mine, other = off_ref[plane], twin_ref[plane]
            for step, peer in enumerate(peers):
                going[step, plane] = (
                    share_ref[band_me, peer] * mine + share_ref[partner, peer] * other
                )
            term_ref[plane] = (
                term_ref[plane]
                + share_ref[band_me, band_me] * mine
                + share_ref[partner, band_me] * other
            )
            return carry

        lax.fori_loop(part * chunk, (part + 1) * chunk, one, 0)
        for copy in chip_copies(part):
            copy.start()

    def home(pair, carry):
        pieces = []
        for which in range(2):
            place = pl.ds((pair * 2 + which) * rows, rows)
            pieces.append(
                jnp.concatenate(
                    [
                        recv_two[half, source, part, place, :]
                        for part in range(2)
                        for source in range(n)
                        for half in range(halves)
                    ],
                    axis=0,
                )
            )
        result = times(fwd_ref[...], jnp.concatenate(pieces, axis=1))
        for which in range(2):
            plane = pair * 2 + which
            lanes = slice(which * length, (which + 1) * length)
            both = jnp.concatenate([result[:length, lanes], result[length:, lanes]], axis=1)
            potential = times(both, bwd_ref[...])
            term_ref[plane] = potential[:, :length] * own_ref[plane]
            off_ref[plane] = potential[:, length:] * second_ref[plane]
        return carry

    for part in range(chunks):
        for copy in back_copies(halves - 1, part):
            copy.wait_send()
        if part + 3 < chunks:
            for copy in back_copies(halves - 1, part + 3):
                copy.start()
        for half in range(halves):
            for copy in back_copies(half, part):
                copy.wait_recv()
        lax.fori_loop(part * chunk // 2, (part + 1) * chunk // 2, home, 0)
        twin_copy(part).start()
        if part > 0:
            shared(part - 1)
    shared(chunks - 1)

    def last(plane, carry):
        total = term_ref[plane]
        for step in range(chips - 1):
            total = total + coming[step, plane]
        term_ref[plane] = total
        return carry

    for part in range(chunks):
        for copy in chip_copies(part):
            copy.wait()
        lax.fori_loop(part * chunk, (part + 1) * chunk, last, 0)
        twin_copy(part).wait_send()
    for part in range(chunks):
        for copy in out_copies(part, halves - 1):
            copy.wait_send()
        for copy in direct_copies(part) + passed_copies(part):
            copy.wait_send()


def exchanged(mix, share, orbital, kernel):
    n = lax.axis_size("grid")
    planes, length = orbital.shape[0], orbital.shape[2]
    chips = lax.axis_size("band") // 2
    depth = length // n
    halves = 2 if depth % 16 == 0 else 1
    rows = depth // halves
    chunk = max(planes // 4, 2)
    chunks = planes // chunk
    forward = complex_table(length)
    vmem = pl.BlockSpec(memory_space=pltpu.VMEM)
    smem = pl.BlockSpec(memory_space=pltpu.SMEM)
    slab = jax.ShapeDtypeStruct(orbital.shape, jnp.float32)
    block = planes * rows
    return pl.pallas_call(
        functools.partial(transform_kernel, n, halves, chunks, chips),
        out_shape=(slab, slab),
        in_specs=[smem] * 2 + [vmem] * 4,
        out_specs=(vmem, vmem),
        scratch_shapes=[
            pltpu.VMEM((n, halves, 2, block, length), jnp.float32),
            pltpu.VMEM((halves, 2, n * block, length), jnp.float32),
            pltpu.VMEM((halves, 2, n * block, length), jnp.float32),
            pltpu.VMEM((halves, n, 2, block, length), jnp.float32),
            pltpu.VMEM(slab.shape, jnp.float32),
            pltpu.VMEM(slab.shape, jnp.float32),
            pltpu.VMEM(slab.shape, jnp.float32),
            pltpu.VMEM((chips - 1,) + slab.shape, jnp.float32),
            pltpu.VMEM((chips - 1,) + slab.shape, jnp.float32),
            pltpu.VMEM((2 * chips,) + slab.shape, jnp.float32),
            pltpu.SemaphoreType.DMA((chunks, halves, n)),
            pltpu.SemaphoreType.DMA((chunks, halves, n)),
            pltpu.SemaphoreType.DMA((chunks, halves, n)),
            pltpu.SemaphoreType.DMA((chunks, halves, n)),
            pltpu.SemaphoreType.DMA((2 * halves,)),
            pltpu.SemaphoreType.DMA((2, chunks)),
            pltpu.SemaphoreType.DMA((2, chunks, max(chips - 1, 1))),
            pltpu.SemaphoreType.DMA((2, chunks, 2 * chips - 1)),
            pltpu.SemaphoreType.DMA((1,)),
        ],
        compiler_params=pltpu.CompilerParams(
            collective_id=0, has_side_effects=True, vmem_limit_bytes=40 * 1024 * 1024
        ),
    )(mix, share, orbital, kernel, jnp.asarray(forward), jnp.asarray(forward.T.copy()))


def assignment(pattern):
    blocks = pattern.shape[0]
    ids = jnp.arange(blocks, dtype=jnp.int32)
    off = ((pattern == 1) & (ids[:, None] != ids[None, :])).astype(jnp.int32).reshape(-1)
    before = jnp.cumsum(off) - off
    chosen = (off[None, :] == 1) & (before[None, :] == ids[:, None])
    chosen = chosen.reshape(blocks, blocks, blocks)
    firsts = jnp.any(chosen, axis=2).astype(jnp.float32)
    seconds = jnp.any(chosen, axis=1).astype(jnp.float32)
    return firsts, seconds


def local(orbitals, pivots, pattern):
    slab_planes = orbitals.shape[1]
    length = orbitals.shape[3]
    block_total = pattern.shape[0]
    grid_index = lax.axis_index("grid")
    band_index = lax.axis_index("band")
    local_cell = pivots - grid_index * (slab_planes * length * length)
    inside = (local_cell >= 0) & (local_cell < slab_planes * length * length)
    cell = jnp.clip(local_cell, 0, slab_planes * length * length - 1)
    rows = jnp.take(orbitals.reshape(slab_planes * length, length), cell // length, axis=0)
    lanes = jnp.arange(length, dtype=jnp.int32)
    sampled = jnp.sum(jnp.where(lanes[None, :] == (cell % length)[:, None], rows, 0.0), axis=1)
    own = jnp.where(inside, sampled, 0.0)
    ids = jnp.arange(block_total, dtype=jnp.int32)
    picked = summed(jnp.where(ids[:, None] == band_index, own[None, :], 0.0))
    gram_matrix = jnp.dot(picked.T, picked, precision=precise)
    factor = jnp.linalg.cholesky(gram_matrix)
    rotation = lax.linalg.triangular_solve(factor, picked.T, left_side=True, lower=True).T
    firsts, seconds = assignment(pattern)
    selectors = jnp.stack(
        [
            (ids == band_index).astype(jnp.float32),
            lax.dynamic_index_in_dim(firsts, band_index, 0, keepdims=False),
            lax.dynamic_index_in_dim(seconds, band_index, 0, keepdims=False),
        ]
    )
    coefficients = jnp.dot(selectors, rotation.T, precision=precise)
    depth = length // lax.axis_size("grid")
    kernel = coulomb(length, grid_index * depth, depth)
    localized, exchange_term = exchanged(coefficients, firsts, orbitals[0], kernel)
    return (localized[None], exchange_term[None])


def solution(mesh):
    return jax.shard_map(
        local,
        mesh=mesh,
        in_specs=(P("band", "grid", None, None), P(), P()),
        out_specs=(P("band", "grid", None, None), P("band", "grid", None, None)),
        check_vma=False,
    )
```
